32 devices in a mesh: wide: 8 (over y, x, core), quad: 4 (over z).
Axes of the slice: x: 2, y: 2, z: 4, core: 2. Of those that a mesh axis runs over, the one named last changes fastest.
Arguments:
- basis: float32 [16, 2097152], P(None, ('wide', 'quad')), may hold values from -6 to 6
- target: float32 [2097152], P(('wide', 'quad')), may hold values from -6 to 6
- sign_bits: int32 [2097152], P(('wide', 'quad')), may hold values from 0 to 1
- samples: int32 [8192], replicated, may hold values from 0 to 2097151
- owners: int32 [8192], replicated, may hold values from 0 to 7
Outputs:
- sketch: float32 [8192, 17], P(('wide', 'quad'))
- gram: float32 [8, 16, 17], P('quad')
The draws below stay inside these ranges and needn't reach their ends.
Inputs may be any that keep to these rules, and one draw needn't show every extreme that they name: `samples`: sampled scenarios may repeat.
All inputs are finite; a program needn't handle non-finite values.
Results may differ from the reference program's by a relative error of at most 0.0003.
Values sent between devices are 32-bit elements; how exact they have to be, the bound alone decides.
A program may use at most 128 MiB of HBM per device.

```python
import math
import jax
import jax.numpy as jnp
import numpy as np
from jax import lax

COLS = 16
ROWS_DEV = 65536
SCEN = 2097152
SAMPLES = 8192
GROUPS = 8
N_WIDE = 8
N_QUAD = 4


def plant(entries, rng, smallest, largest):
    shape = entries.shape
    index_at = [jax.random.randint(jax.random.fold_in(rng, axis), (), 0, shape[axis]) for axis in range(len(shape))]
    entries = entries.at[tuple(index_at)].set(smallest)
    longest = shape.index(max(shape))
    index_at[longest] = (index_at[longest] + 1) % shape[longest]
    return entries.at[tuple(index_at)].set(largest)


def level_of(own_key, shape, cuts, least, high):
    loudness = 1.0
    for axis_at, shards_of in cuts:
        draws = jax.random.uniform(jax.random.fold_in(jax.random.fold_in(own_key, 6), axis_at), (shards_of,), jnp.float32, least / len(cuts), high / len(cuts))
        loudness = loudness * jnp.repeat(jnp.exp(draws), shape[axis_at] // shards_of).reshape((-1,) + (1,) * (len(shape) - 1 - axis_at))
    return loudness


def rank_table(number_of, lean):
    portions = [(1 << 20) // math.isqrt(standing ** lean) + 1 for standing in range(1, number_of + 1)]
    deviation = 1 + sum(portions) // (1 << 30)
    return np.cumsum(np.array([max(1, weight // deviation) for weight in portions]))


def ranked(rng, shape, count, slope):
    table = rank_table(count, slope)
    pick = jax.random.randint(jax.random.fold_in(rng, 1), shape, 0, int(table[count - 1]))
    rank = jnp.searchsorted(jnp.asarray(table, jnp.int32), pick, side="right")
    return jax.random.permutation(jax.random.fold_in(rng, 2), count)[rank].astype(jnp.int32)


def bell_draw(key, shape, scale, reach, cuts=(), kind=jnp.bfloat16):
    drawn = scale * jax.random.normal(key, shape, jnp.float32)
    if cuts:
        drawn = drawn * level_of(key, shape, cuts, -0.22, 0.18)
    return jnp.clip(drawn, -reach, reach).astype(kind)


def setup_inputs(seed: int = 0) -> dict:
    seeds = jax.random.split(jax.random.key(seed), 6)
    return {
        "basis": bell_draw(seeds[0], (COLS, SCEN), 1.0, 6.0, ((1, 32),), jnp.float32),
        "target": bell_draw(seeds[1], (SCEN,), 1.0, 6.0, ((0, 32),), jnp.float32),
        "sign_bits": plant(jax.random.randint(seeds[2], (SCEN,), 0, 2), jax.random.fold_in(seeds[2], 1), 0, 1).astype(jnp.int32),
        "samples": plant(jax.random.randint(seeds[3], (SAMPLES,), 0, SCEN), jax.random.fold_in(seeds[3], 1), 0, SCEN - 1).astype(jnp.int32),
        "owners": plant(ranked(seeds[4], (SAMPLES,), GROUPS, 2), jax.random.fold_in(seeds[4], 3), 0, GROUPS - 1).astype(jnp.int32),
    }


def butterfly(field):
    width, length = field.shape
    half = 1
    while half < length:
        split = field.reshape(width, length // (2 * half), 2, half)
        upper = split[:, :, 0, :]
        lower = split[:, :, 1, :]
        field = jnp.stack([upper + lower, upper - lower], axis=2).reshape(width, length)
        half = half * 2
    return field


def parity_sign(first, second, nbits):
    count = jnp.zeros_like(first)
    for bit in range(nbits):
        count = count + ((first & second) >> bit) & 1
    return (1 - 2 * (count & 1)).astype(jnp.float32)


def reference(basis, target, sign_bits, samples, owners):
    devices = N_WIDE * N_QUAD
    rows = ROWS_DEV
    nbits = devices.bit_length() - 1
    dev_of = (samples // rows).astype(jnp.int32)
    pos_of = (samples % rows).astype(jnp.int32)
    scale = 1.0 / float(SCEN) ** 0.5

    def step(carry, dev):
        start = (dev * rows).astype(jnp.int32)
        part_basis = lax.dynamic_slice_in_dim(basis, start, rows, 1)
        part_target = lax.dynamic_slice_in_dim(target, start, rows, 0)
        part_bits = lax.dynamic_slice_in_dim(sign_bits, start, rows, 0)
        flip = (1 - 2 * part_bits).astype(jnp.float32)
        signed = jnp.concatenate([part_basis, part_target[None, :]], axis=0) * flip[None, :]
        local = butterfly(signed)
        values = jnp.take(local, pos_of, axis=1)
        sign = parity_sign(dev_of, jnp.full_like(dev_of, dev), nbits)
        return carry + values * sign[None, :], None

    init = jnp.zeros((COLS + 1, SAMPLES), jnp.float32)
    total, _ = lax.scan(step, init, jnp.arange(devices, dtype=jnp.int32))
    sketch = (total * scale).T
    onehot = (owners[:, None] == jnp.arange(GROUPS, dtype=jnp.int32)[None, :]).astype(jnp.float32)
    gram = jnp.einsum("rg,ri,rj->gij", onehot, sketch[:, :COLS], sketch, precision=lax.Precision.HIGHEST)
    gram = gram * (GROUPS / SAMPLES)
    return sketch, gram
```

```python
import functools
import math

import jax
import jax.numpy as jnp
from jax import lax
from jax.experimental import pallas as pl
from jax.experimental.pallas import tpu as pltpu
from jax.sharding import PartitionSpec as P

GROUPS = 8
LANES = 128
LINE = 256
HIGH = 8
SLOT = 32
MESH = pl.DeviceIdType.MESH


def bits_of(n):
    return n.bit_length() - 1


def parity(x, nbits):
    shift = 1
    while shift < nbits:
        x = x ^ (x >> shift)
        shift *= 2
    return x & 1


def butterfly(parts):
    half = 1
    while half < len(parts):
        for at in range(0, len(parts), 2 * half):
            for i in range(at, at + half):
                parts[i], parts[i + half] = parts[i] + parts[i + half], parts[i] - parts[i + half]
        half *= 2
    return parts


def place_of(high):
    return ((high & 1) * (HIGH // 2) + (high >> 1)) * SLOT


def split(x):
    top = x.astype(jnp.bfloat16)
    return top, (x - top.astype(jnp.float32)).astype(jnp.bfloat16)


def contract_last(a, b, **kw):
    return lax.dot_general(a, b, (((1,), (1,)), ((), ())), preferred_element_type=jnp.float32, **kw)


def transform_kernel(
    n_wide, n_quad, scale, picks, samp, bits, x, t, main, last, field, table, walsh, unit, picked
):
    high = pl.program_id(0)
    cols, chunk = x.shape
    mids = chunk // LINE
    local_bits = bits_of(HIGH * chunk)
    per_dev = main.shape[2]
    devices = n_wide * n_quad

    @pl.when(high == 0)
    def _():
        a = lax.broadcasted_iota(jnp.int32, (LINE, LINE), 0)
        b = lax.broadcasted_iota(jnp.int32, (LINE, LINE), 1)
        walsh[...] = (1 - 2 * parity(a & b, bits_of(LINE))).astype(jnp.float32).astype(jnp.bfloat16)
        a = lax.broadcasted_iota(jnp.int32, (LANES, LANES), 0)
        b = lax.broadcasted_iota(jnp.int32, (LANES, LANES), 1)
        unit[...] = jnp.where(a == b, 1.0, 0.0).astype(jnp.bfloat16)

    row = lax.broadcasted_iota(jnp.int32, (8, LANES), 0)
    base = pl.multiple_of(place_of(high), SLOT)
    for part in range(LINE // LANES):
        for tile in range(cols // 8 + 1):
            values = []
            for mid in range(mids):
                line = mid * (LINE // LANES) + part
                flip = (1 - 2 * bits[line : line + 1, :]).astype(jnp.float32)
                if tile < cols // 8:
                    value = x[tile * 8 : tile * 8 + 8, line * LANES : (line + 1) * LANES] * flip
                else:
                    value = jnp.where(row == 0, t[line : line + 1, :] * flip, 0.0)
                values.append(value)
            for mid, value in enumerate(butterfly(values)):
                field[mid, pl.ds(base + tile * 8, 8), part * LANES : (part + 1) * LANES] = value

    @pl.when(high == HIGH - 1)
    def _():
        used = cols + 8

        def mix(mid, carry):
            halves = []
            for part in range(LINE // LANES):
                values = [
                    field[mid, place_of(h) : place_of(h) + used, part * LANES : (part + 1) * LANES]
                    for h in range(HIGH)
                ]
                values = butterfly(values)
                order = sorted(range(HIGH), key=place_of)
                blank = jnp.zeros((SLOT - used, LANES), jnp.float32)
                halves.append(jnp.concatenate([p for h in order for p in (values[h], blank)], axis=0))
            top, low = split(jnp.concatenate(halves, axis=1))
            out = contract_last(walsh[...], top) + contract_last(walsh[...], low)
            at = pl.multiple_of(mid * LINE, LINE)
            table[pl.ds(at, LINE), :] = out[:, :LANES]
            table[pl.ds(at + mids * LINE, LINE), :] = out[:, LANES:]
            return carry

        lax.fori_loop(0, mids, mix, 0)
        me = lax.axis_index("wide") * n_quad + lax.axis_index("quad")
        table_rows = table.shape[0]

        def gather(slot, carry):
            wide = slot // n_quad
            turned = jnp.int32(0)
            for bit in range(bits_of(n_wide)):
                turned = turned * 2 + ((wide >> bit) & 1)
            dev = turned * n_quad + slot % n_quad
            start = dev * per_dev
            for r in range(per_dev):
                at = picks[start + r] & (table_rows - 1)
                picked[r : r + 1, :] = table[pl.ds(at, 1), :]
            top, low = split(picked[...])
            out = contract_last(unit[...], top) + contract_last(unit[...], low)
            lines = per_dev // LANES
            number = jnp.concatenate(
                [samp[pl.ds(dev * lines + i, 1), :] for i in range(lines)], axis=1
            )
            group = (number >> bits_of(table_rows)) & (LANES // SLOT - 1)
            sign = parity((number >> local_bits) & me, bits_of(devices))
            sign = (1 - 2 * sign).astype(jnp.float32) * scale
            total = jnp.zeros((used, per_dev), jnp.float32)
            for g in range(LANES // SLOT):
                total = jnp.where(group == g, out[g * SLOT : g * SLOT + used, :], total)
            total = total * sign
            main[slot] = total[:cols]
            for i in range(lines):
                last[pl.ds(slot * lines + i, 1), :] = total[cols : cols + 1, i * LANES : (i + 1) * LANES]
            return carry

        lax.fori_loop(0, devices, gather, 0)


def reduce_kernel(n_wide, n_quad, total_samples, main, last, owners, sketch, gram, *scratch):
    steps = bits_of(n_wide)
    got_main, scratch = scratch[:steps], scratch[steps:]
    got_last, scratch = scratch[:steps], scratch[steps:]
    sum_main, scratch = scratch[:steps], scratch[steps:]
    sum_last, scratch = scratch[:steps], scratch[steps:]
    quad_main, quad_last, gram_own, gram_got, quad_gram, turned, sends, recvs = scratch
    wide = lax.axis_index("wide")
    quad = lax.axis_index("quad")
    me = wide * n_quad + quad
    devices, cols, per_dev = main.shape
    lines = per_dev // LANES
    pairs = [(wide + (1 << k) - 2 * (1 << k) * ((wide // (1 << k)) % 2), quad) for k in range(steps)]
    rows = [(wide, (quad + k) % n_quad) for k in range(1, n_quad)]

    barrier = pltpu.get_barrier_semaphore()
    for peer in pairs + rows:
        pl.semaphore_signal(barrier, inc=1, device_id=peer, device_id_type=MESH)
    pl.semaphore_wait(barrier, len(pairs) + len(rows))

    used = [0]

    def send(src, dst, peer):
        sem = used[0]
        used[0] += 1
        copy = pltpu.make_async_remote_copy(
            src_ref=src, dst_ref=dst, send_sem=sends.at[sem], recv_sem=recvs.at[sem],
            device_id=peer, device_id_type=MESH,
        )
        copy.start()
        return copy

    now_main, now_last = main, last
    pending = []
    copies = []
    size = devices
    for k in range(steps):
        size //= 2
        bit = (wide // (1 << k)) % 2
        give, keep = (1 - bit) * size, bit * size
        if k:
            add_up(now_main, now_last, before, give, size, lines)
        copies = [
            send(now_main.at[pl.ds(give, size)], got_main[k], pairs[k]),
            send(now_last.at[pl.ds(pl.multiple_of(give * lines, 8), size * lines)], got_last[k], pairs[k]),
        ]
        if k:
            add_up(now_main, now_last, before, keep, size, lines)
        for copy in copies:
            copy.wait()
        before = (now_main, now_last, got_main[k], got_last[k], keep)
        now_main, now_last = sum_main[k], sum_last[k]
    for k in range(1, n_quad):
        add_up(now_main, now_last, before, (quad + k) % n_quad, 1, 0)
    add_up(now_main, now_last, before, 0, n_quad, lines, False)
    copies = []
    for k, peer in enumerate(rows):
        copies.append(send(now_main.at[peer[1]], quad_main.at[k], peer))
        copies.append(send(now_last, quad_last.at[k], peer))
    add_up(now_main, now_last, before, quad, 1, 0)
    for copy in copies:
        copy.wait()
    total = now_main[quad]
    ends = [now_last[pl.ds(quad * lines + i, 1), :] for i in range(lines)]
    for k in range(n_quad - 1):
        total = total + quad_main[k]
        ends = [e + quad_last[k, pl.ds(quad * lines + i, 1), :] for i, e in enumerate(ends)]
    end = jnp.concatenate(ends, axis=1)
    sketch[:cols, :] = total
    sketch[cols : cols + 1, :] = end

    group = jnp.concatenate([owners[pl.ds(me * lines + i, 1), :] for i in range(lines)], axis=1)
    row = lax.broadcasted_iota(jnp.int32, (8, per_dev), 0)
    right = jnp.concatenate([total, jnp.where(row == 0, end, 0.0)], axis=0)
    left = jnp.concatenate([jnp.where(group == g, total, 0.0) for g in range(GROUPS)], axis=0)
    part = contract_last(right, left, precision=lax.Precision.HIGHEST)
    part = part * (GROUPS / total_samples)
    for k in range(steps):
        gram_own[k] = part
        copy = send(gram_own.at[k], gram_got.at[k], pairs[k])
        copy.wait()
        part = part + gram_got[k]
    gram_own[steps] = part
    copies = [send(gram_own.at[steps], quad_gram.at[k], peer) for k, peer in enumerate(rows)]
    for copy in copies:
        copy.wait()
    for k in range(n_quad - 1):
        part = part + quad_gram[k]
    turned[:, : part.shape[0]] = part.T
    owned = GROUPS // n_quad
    for g in range(owned):
        gram[g] = turned[pl.ds((quad * owned + g) * cols, cols), : cols + 1]


def add_up(out_main, out_last, before, start, size, lines, whole=True):
    main, last, got_main, got_last, keep = before
    if whole:
        out_main[pl.ds(start, size)] = main[pl.ds(keep + start, size)] + got_main[pl.ds(start, size)]
    if lines:
        to = pl.multiple_of(start * lines, 8)
        at = pl.multiple_of((keep + start) * lines, 8)
        out_last[pl.ds(to, size * lines), :] = (
            last[pl.ds(at, size * lines), :] + got_last[pl.ds(to, size * lines), :]
        )


def shards(n_wide, n_quad, basis, target, sign_bits, samples, owners):
    cols, rows = basis.shape
    devices = n_wide * n_quad
    total_samples = samples.shape[0]
    per_dev = total_samples // devices
    lines = per_dev // LANES
    scale = 1.0 / math.sqrt(rows * devices)
    chunk = rows // HIGH
    mids = chunk // LINE
    vmem = pl.BlockSpec(memory_space=pltpu.VMEM)
    f32 = jnp.float32
    main, last = pl.pallas_call(
        functools.partial(transform_kernel, n_wide, n_quad, scale),
        grid=(HIGH,),
        out_shape=(
            jax.ShapeDtypeStruct((devices, cols, per_dev), f32),
            jax.ShapeDtypeStruct((devices * lines, LANES), f32),
        ),
        in_specs=[
            pl.BlockSpec(memory_space=pltpu.SMEM),
            vmem,
            pl.BlockSpec((chunk // LANES, LANES), lambda h: (h, 0)),
            pl.BlockSpec((cols, chunk), lambda h: (0, h)),
            pl.BlockSpec((chunk // LANES, LANES), lambda h: (h, 0)),
        ],
        out_specs=(vmem, vmem),
        scratch_shapes=[
            pltpu.VMEM((mids, HIGH * SLOT, LINE), f32),
            pltpu.VMEM((rows * SLOT // LANES, LANES), f32),
            pltpu.VMEM((LINE, LINE), jnp.bfloat16),
            pltpu.VMEM((LANES, LANES), jnp.bfloat16),
            pltpu.VMEM((per_dev, LANES), f32),
        ],
        compiler_params=pltpu.CompilerParams(vmem_limit_bytes=60 * 1024 * 1024),
    )(
        samples,
        samples.reshape(-1, LANES),
        sign_bits.reshape(-1, LANES),
        basis,
        target.reshape(-1, LANES),
    )

    steps = bits_of(n_wide)
    sizes = [devices >> (k + 1) for k in range(steps)]
    mains = [pltpu.VMEM((s, cols, per_dev), f32) for s in sizes]
    lasts = [pltpu.VMEM((s * lines, LANES), f32) for s in sizes]
    copies = 3 * steps + 3 * (n_quad - 1)
    wide_gram = GROUPS * cols
    tall = cols + 8
    sketch, gram = pl.pallas_call(
        functools.partial(reduce_kernel, n_wide, n_quad, total_samples),
        out_shape=(
            jax.ShapeDtypeStruct((cols + 1, per_dev), f32),
            jax.ShapeDtypeStruct((GROUPS // n_quad, cols, cols + 1), f32),
        ),
        in_specs=[vmem, vmem, vmem],
        out_specs=(vmem, vmem),
        scratch_shapes=mains + lasts + mains + lasts + [
            pltpu.VMEM((n_quad - 1, cols, per_dev), f32),
            pltpu.VMEM((n_quad - 1, n_quad * lines, LANES), f32),
            pltpu.VMEM((steps + 1, tall, wide_gram), f32),
            pltpu.VMEM((steps, tall, wide_gram), f32),
            pltpu.VMEM((n_quad - 1, tall, wide_gram), f32),
            pltpu.VMEM((wide_gram, LANES), f32),
            pltpu.SemaphoreType.DMA((copies,)),
            pltpu.SemaphoreType.DMA((copies,)),
        ],
        compiler_params=pltpu.CompilerParams(collective_id=0, has_side_effects=True),
    )(main, last, owners.reshape(-1, LANES))
    return sketch.T, gram


def solution(mesh):
    placed = (P(None, ("wide", "quad")), P(("wide", "quad")), P(("wide", "quad")), P(), P())
    return jax.shard_map(
        functools.partial(shards, mesh.shape["wide"], mesh.shape["quad"]),
        mesh=mesh,
        in_specs=placed,
        out_specs=(P(("wide", "quad"), None), P("quad", None, None)),
        check_vma=False,
    )
```

```python
import functools
import math

import jax
import jax.numpy as jnp
from jax import lax
from jax.experimental import pallas as pl
from jax.experimental.pallas import tpu as pltpu
from jax.sharding import PartitionSpec as P

GROUPS = 8
LANES = 128
LINE = 256
HIGH = 8
SLOT = 32
MESH = pl.DeviceIdType.MESH


def bits_of(n):
    return n.bit_length() - 1


def parity(x, nbits):
    shift = 1
    while shift < nbits:
        x = x ^ (x >> shift)
        shift *= 2
    return x & 1


def butterfly(parts):
    half = 1
    while half < len(parts):
        for at in range(0, len(parts), 2 * half):
            for i in range(at, at + half):
                parts[i], parts[i + half] = parts[i] + parts[i + half], parts[i] - parts[i + half]
        half *= 2
    return parts


def place_of(high):
    return ((high & 1) * (HIGH // 2) + (high >> 1)) * SLOT


def split(x):
    top = x.astype(jnp.bfloat16)
    return top, (x - top.astype(jnp.float32)).astype(jnp.bfloat16)


def contract_last(a, b, **kw):
    return lax.dot_general(a, b, (((1,), (1,)), ((), ())), preferred_element_type=jnp.float32, **kw)


def transform_kernel(
    n_wide, n_quad, scale, samp, bits, x, t, main, last, field, table, walsh, unit,
    picks, picks_a, picks_b, rows_a, rows_b, sems
):
    high = pl.program_id(0)
    cols, chunk = x.shape
    mids = chunk // LINE
    local_bits = bits_of(HIGH * chunk)
    per_dev = main.shape[2]
    devices = n_wide * n_quad

    @pl.when(high == 0)
    def _():
        a = lax.broadcasted_iota(jnp.int32, (LINE, LINE), 0)
        b = lax.broadcasted_iota(jnp.int32, (LINE, LINE), 1)
        line = (1 - 2 * parity(a & b, bits_of(LINE))).astype(jnp.float32).astype(jnp.bfloat16)
        walsh[:, :LINE] = line
        walsh[:, LINE:] = line
        a = lax.broadcasted_iota(jnp.int32, (LANES, LANES), 0)
        b = lax.broadcasted_iota(jnp.int32, (LANES, LANES), 1)
        line = jnp.where(a == b, 1.0, 0.0).astype(jnp.bfloat16)
        unit[:, :LANES] = line
        unit[:, LANES:] = line
        picks[...] = samp[...] & (table.shape[0] - 1)

    row = lax.broadcasted_iota(jnp.int32, (8, LANES), 0)
    base = pl.multiple_of(place_of(high), SLOT)
    for part in range(LINE // LANES):
        for tile in range(cols // 8 + 1):
            values = []
            for mid in range(mids):
                line = mid * (LINE // LANES) + part
                flip = (1 - 2 * bits[line : line + 1, :]).astype(jnp.float32)
                if tile < cols // 8:
                    value = x[tile * 8 : tile * 8 + 8, line * LANES : (line + 1) * LANES] * flip
                else:
                    value = jnp.where(row == 0, t[line : line + 1, :] * flip, 0.0)
                values.append(value)
            for mid, value in enumerate(butterfly(values)):
                field[mid, pl.ds(base + tile * 8, 8), part * LANES : (part + 1) * LANES] = value

    @pl.when(high == HIGH - 1)
    def _():
        used = cols + 8

        def mix(mid, carry):
            halves = []
            for part in range(LINE // LANES):
                values = [
                    field[mid, place_of(h) : place_of(h) + used, part * LANES : (part + 1) * LANES]
                    for h in range(HIGH)
                ]
                values = butterfly(values)
                order = sorted(range(HIGH), key=place_of)
                blank = jnp.zeros((SLOT - used, LANES), jnp.float32)
                halves.append(jnp.concatenate([p for h in order for p in (values[h], blank)], axis=0))
            both = jnp.concatenate(split(jnp.concatenate(halves, axis=1)), axis=1)
            out = contract_last(walsh[...], both)
            at = pl.multiple_of(mid * LINE, LINE)
            table[pl.ds(at, LINE), :] = out[:, :LANES]
            table[pl.ds(at + mids * LINE, LINE), :] = out[:, LANES:]
            return carry

        lax.fori_loop(0, mids, mix, 0, unroll=2)
        me = lax.axis_index("wide") * n_quad + lax.axis_index("quad")
        table_rows = table.shape[0]
        lines = per_dev // LANES
        inner = devices // 2

        def device_at(slot):
            wide = (slot // n_quad) % (n_wide // 2) * 2 + slot // inner
            return wide * n_quad + slot % n_quad

        def fetch(slot, slots, sem):
            slot = jnp.minimum(slot, devices - 1)
            return pltpu.make_async_copy(picks.at[device_at(slot)], slots, sems.at[sem])

        def gather(slots, rows):
            for r in range(per_dev):
                rows[r : r + 1, :] = table[pl.ds(slots[r // LANES, r % LANES], 1), :]

        def finish(slot, rows):
            dev = device_at(slot)
            out = contract_last(unit[...], jnp.concatenate(split(rows[...]), axis=1))
            number = jnp.concatenate([samp[dev, i : i + 1] for i in range(lines)], axis=1)
            group = (number >> bits_of(table_rows)) & (LANES // SLOT - 1)
            sign = parity((number >> local_bits) & me, bits_of(devices))
            sign = (1 - 2 * sign).astype(jnp.float32) * scale
            total = jnp.zeros((used, per_dev), jnp.float32)
            for g in range(LANES // SLOT):
                total = jnp.where(group == g, out[g * SLOT : g * SLOT + used, :], total)
            total = total * sign
            main[slot] = total[:cols]
            for i in range(lines):
                last[pl.ds(slot * lines + i, 1), :] = total[cols : cols + 1, i * LANES : (i + 1) * LANES]

        fetch(0, picks_a, 0).start()
        fetch(1, picks_b, 1).start()
        fetch(0, picks_a, 0).wait()
        gather(picks_a, rows_a)
        fetch(2, picks_a, 0).start()

        def pair(i, carry):
            slot = 2 * i
            fetch(slot + 1, picks_b, 1).wait()
            gather(picks_b, rows_b)
            finish(slot, rows_a)
            fetch(slot + 3, picks_b, 1).start()
            fetch(slot + 2, picks_a, 0).wait()
            gather(picks_a, rows_a)
            finish(slot + 1, rows_b)
            fetch(slot + 4, picks_a, 0).start()
            return carry

        lax.fori_loop(0, devices // 2, pair, 0)
        fetch(0, picks_a, 0).wait()
        fetch(0, picks_b, 1).wait()


def reduce_kernel(
    n_wide, n_quad, total_samples, main, last, owners, sketch, gram,
    got_main, got_last, sum_main, sum_last, wide_main, wide_last, row_main, row_last,
    quad_main, quad_last, wide_gram, own_gram, quad_gram, sends, recvs
):
    wide = lax.axis_index("wide")
    quad = lax.axis_index("quad")
    me = wide * n_quad + quad
    devices, cols, per_dev = main.shape
    lines = per_dev // LANES
    core, chip, chips = wide % 2, wide // 2, n_wide // 2
    mate = (wide + 1 - 2 * core, quad)
    chip_peers = [(chip + k) % chips for k in range(1, chips)]
    wide_peers = [((wide + k) % n_wide, quad) for k in range(1, n_wide)]
    quad_peers = [(wide, (quad + k) % n_quad) for k in range(1, n_quad)]

    barrier = pltpu.get_barrier_semaphore()
    for peer in wide_peers + quad_peers:
        pl.semaphore_signal(barrier, inc=1, device_id=peer, device_id_type=MESH)
    pl.semaphore_wait(barrier, len(wide_peers) + len(quad_peers))

    used = [0]

    def send(src, dst, peer):
        sem = used[0]
        used[0] += 1
        copy = pltpu.make_async_remote_copy(
            src_ref=src, dst_ref=dst, send_sem=sends.at[sem], recv_sem=recvs.at[sem],
            device_id=peer, device_id_type=MESH,
        )
        copy.start()
        return copy

    half = devices // 2
    tall = n_quad * lines
    give, keep = (1 - core) * half, core * half
    copies = [
        send(main.at[pl.ds(give, half)], got_main, mate),
        send(last.at[pl.ds(pl.multiple_of(give * lines, 8), half * lines)], got_last, mate),
    ]
    for copy in copies:
        copy.wait()

    def add(to):
        at = pl.ds(to * n_quad, n_quad)
        sum_main[at] = main[pl.ds(keep + to * n_quad, n_quad)] + got_main[at]
        at = pl.ds(pl.multiple_of(to * tall, 8), tall)
        from_at = pl.ds(pl.multiple_of(keep * lines + to * tall, 8), tall)
        sum_last[at, :] = last[from_at, :] + got_last[at, :]

    copies = []
    for k, peer in enumerate(chip_peers):
        add(peer)
        there = (peer * 2 + core, quad)
        copies.append(send(sum_main.at[pl.ds(peer * n_quad, n_quad)], wide_main.at[k], there))
        copies.append(
            send(sum_last.at[pl.ds(pl.multiple_of(peer * tall, 8), tall)], wide_last.at[k], there)
        )
    add(chip)
    for copy in copies:
        copy.wait()

    def add_row(to):
        row = sum_main[chip * n_quad + to]
        for k in range(chips - 1):
            row = row + wide_main[k, to]
        row_main[to] = row

    ends = sum_last[pl.ds(pl.multiple_of(chip * tall, 8), tall), :]
    for k in range(chips - 1):
        ends = ends + wide_last[k]
    row_last[...] = ends
    copies = []
    for k, peer in enumerate(quad_peers):
        add_row(peer[1])
        copies.append(send(row_main.at[peer[1]], quad_main.at[k], peer))
        copies.append(send(row_last, quad_last.at[k], peer))
    add_row(quad)
    for copy in copies:
        copy.wait()
    total = row_main[quad]
    ends = [row_last[pl.ds(quad * lines + i, 1), :] for i in range(lines)]
    for k in range(n_quad - 1):
        total = total + quad_main[k]
        ends = [e + quad_last[k, pl.ds(quad * lines + i, 1), :] for i, e in enumerate(ends)]
    end = jnp.concatenate(ends, axis=1)
    sketch[:cols, :] = total
    sketch[cols : cols + 1, :] = end

    group = jnp.concatenate([owners[me, i : i + 1] for i in range(lines)], axis=1)
    row = lax.broadcasted_iota(jnp.int32, (8, per_dev), 0)
    right = jnp.concatenate([total, jnp.where(row == 0, end, 0.0)], axis=0)
    left = jnp.concatenate([jnp.where(group == g, total, 0.0) for g in range(GROUPS)], axis=0)
    part = contract_last(right, left, precision=lax.Precision.HIGHEST)
    wide_gram[0] = part * (GROUPS / total_samples)
    copies = [send(wide_gram.at[0], wide_gram.at[k + 1], peer) for k, peer in enumerate(wide_peers)]
    for copy in copies:
        copy.wait()
    part = wide_gram[wide]
    for w in range(1, n_wide):
        part = part + wide_gram[(wide + n_wide - w) % n_wide]
    own_gram[...] = part
    copies = [send(own_gram, quad_gram.at[k], peer) for k, peer in enumerate(quad_peers)]
    for copy in copies:
        copy.wait()
    for k in range(n_quad - 1):
        part = part + quad_gram[k]
    gram[...] = part


def finish_kernel(n_quad, sketch_in, gram_in, sketch, gram, turned):
    quad = lax.axis_index("quad")
    owned, cols, _ = gram.shape
    sketch[...] = sketch_in[...]
    turned[:, : gram_in.shape[0]] = gram_in[...].T
    for g in range(owned):
        gram[g] = turned[pl.ds((quad * owned + g) * cols, cols), : cols + 1]


def shards(n_wide, n_quad, basis, target, sign_bits, samples, owners):
    cols, rows = basis.shape
    devices = n_wide * n_quad
    total_samples = samples.shape[0]
    per_dev = total_samples // devices
    lines = per_dev // LANES
    scale = 1.0 / math.sqrt(rows * devices)
    chunk = rows // HIGH
    mids = chunk // LINE
    vmem = pl.BlockSpec(memory_space=pltpu.VMEM)
    f32 = jnp.float32
    main, last = pl.pallas_call(
        functools.partial(transform_kernel, n_wide, n_quad, scale),
        grid=(HIGH,),
        out_shape=(
            jax.ShapeDtypeStruct((devices, cols, per_dev), f32),
            jax.ShapeDtypeStruct((devices * lines, LANES), f32),
        ),
        in_specs=[
            vmem,
            pl.BlockSpec((chunk // LANES, LANES), lambda h: (h, 0)),
            pl.BlockSpec((cols, chunk), lambda h: (0, h)),
            pl.BlockSpec((chunk // LANES, LANES), lambda h: (h, 0)),
        ],
        out_specs=(vmem, vmem),
        scratch_shapes=[
            pltpu.VMEM((mids, HIGH * SLOT, LINE), f32),
            pltpu.VMEM((rows * SLOT // LANES, LANES), f32),
            pltpu.VMEM((LINE, 2 * LINE), jnp.bfloat16),
            pltpu.VMEM((LANES, 2 * LANES), jnp.bfloat16),
            pltpu.VMEM((devices, lines, LANES), jnp.int32),
            pltpu.SMEM((lines, LANES), jnp.int32),
            pltpu.SMEM((lines, LANES), jnp.int32),
            pltpu.VMEM((per_dev, LANES), f32),
            pltpu.VMEM((per_dev, LANES), f32),
            pltpu.SemaphoreType.DMA((2,)),
        ],
        compiler_params=pltpu.CompilerParams(vmem_limit_bytes=60 * 1024 * 1024),
    )(
        samples.reshape(devices, lines, LANES),
        sign_bits.reshape(-1, LANES),
        basis,
        target.reshape(-1, LANES),
    )

    half, chips = devices // 2, n_wide // 2
    copies = 2 * chips + 2 * (n_quad - 1) + n_wide - 1 + n_quad - 1
    flat = (cols + 8, GROUPS * cols)
    spaces = [
        (half, cols, per_dev), (half * lines, LANES),
        (half, cols, per_dev), (half * lines, LANES),
        (chips - 1, n_quad, cols, per_dev), (chips - 1, n_quad * lines, LANES),
        (n_quad, cols, per_dev), (n_quad * lines, LANES),
        (n_quad - 1, cols, per_dev), (n_quad - 1, n_quad * lines, LANES),
        (n_wide, *flat), flat, (n_quad - 1, *flat),
    ]
    sketch, gram = pl.pallas_call(
        functools.partial(reduce_kernel, n_wide, n_quad, total_samples),
        out_shape=(
            jax.ShapeDtypeStruct((cols + 1, per_dev), f32),
            jax.ShapeDtypeStruct(flat, f32),
        ),
        in_specs=[vmem, vmem, vmem],
        out_specs=(vmem, vmem),
        scratch_shapes=[pltpu.VMEM(space, f32) for space in spaces]
        + [pltpu.SemaphoreType.DMA((copies,))] * 2,
        compiler_params=pltpu.CompilerParams(collective_id=0, has_side_effects=True),
    )(main, last, owners.reshape(devices, lines, LANES))
    sketch, gram = pl.pallas_call(
        functools.partial(finish_kernel, n_quad),
        out_shape=(
            jax.ShapeDtypeStruct((cols + 1, per_dev), f32),
            jax.ShapeDtypeStruct((GROUPS // n_quad, cols, cols + 1), f32),
        ),
        in_specs=[vmem, vmem],
        out_specs=(vmem, vmem),
        scratch_shapes=[pltpu.VMEM((GROUPS * cols, LANES), f32)],
    )(sketch, gram)
    return sketch.T, gram


def solution(mesh):
    placed = (P(None, ("wide", "quad")), P(("wide", "quad")), P(("wide", "quad")), P(), P())
    return jax.shard_map(
        functools.partial(shards, mesh.shape["wide"], mesh.shape["quad"]),
        mesh=mesh,
        in_specs=placed,
        out_specs=(P(("wide", "quad"), None), P("quad", None, None)),
        check_vma=False,
    )
```

```python
import functools
import math

import jax
import jax.numpy as jnp
from jax import lax
from jax.experimental import pallas as pl
from jax.experimental.pallas import tpu as pltpu
from jax.sharding import PartitionSpec as P

GROUPS = 8
LANES = 128
LINE = 256
HIGH = 8
SLOT = 32
MESH = pl.DeviceIdType.MESH


def bits_of(n):
    return n.bit_length() - 1


def parity(x, nbits):
    shift = 1
    while shift < nbits:
        x = x ^ (x >> shift)
        shift *= 2
    return x & 1


def butterfly(parts):
    half = 1
    while half < len(parts):
        for at in range(0, len(parts), 2 * half):
            for i in range(at, at + half):
                parts[i], parts[i + half] = parts[i] + parts[i + half], parts[i] - parts[i + half]
        half *= 2
    return parts


def place_of(high):
    return ((high & 1) * (HIGH // 2) + (high >> 1)) * SLOT


def split(x):
    top = x.astype(jnp.bfloat16)
    return top, (x - top.astype(jnp.float32)).astype(jnp.bfloat16)


def contract_last(a, b, **kw):
    return lax.dot_general(a, b, (((1,), (1,)), ((), ())), preferred_element_type=jnp.float32, **kw)


def sketch_kernel(
    n_wide, n_quad, scale, samp, owners, bits, x, t, sketch, gram,
    field, table, walsh, unit, picks, picks_a, picks_b, rows_a, rows_b, sems,
    main, last, got_main, got_last, sum_main, sum_last, wide_main, wide_last,
    row_main, row_last, quad_main, quad_last, wide_gram, own_gram, quad_gram,
    mate_sends, mate_recvs, chip_sends, chip_recvs, sends, recvs
):
    high = pl.program_id(0)
    chunk = x.shape[1]
    mids = chunk // LINE
    local_bits = bits_of(HIGH * chunk)
    devices, cols, per_dev = main.shape
    lines = per_dev // LANES
    wide = lax.axis_index("wide")
    quad = lax.axis_index("quad")
    me = wide * n_quad + quad
    core, chip, chips = wide % 2, wide // 2, n_wide // 2
    mate = (wide + 1 - 2 * core, quad)
    wide_peers = [((wide + k) % n_wide, quad) for k in range(1, n_wide)]
    quad_peers = [(wide, (quad + k) % n_quad) for k in range(1, n_quad)]
    barrier = pltpu.get_barrier_semaphore()

    @pl.when(high == 0)
    def _():
        for peer in wide_peers + quad_peers:
            pl.semaphore_signal(barrier, inc=1, device_id=peer, device_id_type=MESH)
        a = lax.broadcasted_iota(jnp.int32, (LINE, LINE), 0)
        b = lax.broadcasted_iota(jnp.int32, (LINE, LINE), 1)
        line = (1 - 2 * parity(a & b, bits_of(LINE))).astype(jnp.float32).astype(jnp.bfloat16)
        walsh[:, :LINE] = line
        walsh[:, LINE:] = line
        a = lax.broadcasted_iota(jnp.int32, (LANES, LANES), 0)
        b = lax.broadcasted_iota(jnp.int32, (LANES, LANES), 1)
        line = jnp.where(a == b, 1.0, 0.0).astype(jnp.bfloat16)
        unit[:, :LANES] = line
        unit[:, LANES:] = line
        picks[...] = samp[...] & (table.shape[0] - 1)

    row = lax.broadcasted_iota(jnp.int32, (8, LANES), 0)
    base = pl.multiple_of(place_of(high), SLOT)
    for part in range(LINE // LANES):
        for tile in range(cols // 8 + 1):
            values = []
            for mid in range(mids):
                line = mid * (LINE // LANES) + part
                flip = (1 - 2 * bits[line : line + 1, :]).astype(jnp.float32)
                if tile < cols // 8:
                    value = x[tile * 8 : tile * 8 + 8, line * LANES : (line + 1) * LANES] * flip
                else:
                    value = jnp.where(row == 0, t[line : line + 1, :] * flip, 0.0)
                values.append(value)
            for mid, value in enumerate(butterfly(values)):
                field[mid, pl.ds(base + tile * 8, 8), part * LANES : (part + 1) * LANES] = value

    @pl.when(high == HIGH - 1)
    def _():
        used = cols + 8

        def mix(mid, carry):
            halves = []
            for part in range(LINE // LANES):
                values = [
                    field[mid, place_of(h) : place_of(h) + used, part * LANES : (part + 1) * LANES]
                    for h in range(HIGH)
                ]
                values = butterfly(values)
                order = sorted(range(HIGH), key=place_of)
                blank = jnp.zeros((SLOT - used, LANES), jnp.float32)
                halves.append(jnp.concatenate([p for h in order for p in (values[h], blank)], axis=0))
            both = jnp.concatenate(split(jnp.concatenate(halves, axis=1)), axis=1)
            out = contract_last(walsh[...], both)
            at = pl.multiple_of(mid * LINE, LINE)
            table[pl.ds(at, LINE), :] = out[:, :LANES]
            table[pl.ds(at + mids * LINE, LINE), :] = out[:, LANES:]
            return carry

        lax.fori_loop(0, mids, mix, 0, unroll=2)
        table_rows = table.shape[0]
        half = devices // 2

        def chip_at(k):
            return (chip + 1 + k) % chips

        def device_at(slot):
            to_core = (core + 1 + slot // half) % 2
            to_wide = chip_at(slot // n_quad % chips) * 2 + to_core
            return to_wide * n_quad + slot % n_quad

        def fetch(slot, slots, sem):
            slot = jnp.minimum(slot, devices - 1)
            return pltpu.make_async_copy(picks.at[device_at(slot)], slots, sems.at[sem])

        def gather(slots, rows):
            for r in range(per_dev):
                rows[r : r + 1, :] = table[pl.ds(slots[r // LANES, r % LANES], 1), :]

        def finish(slot, rows):
            dev = device_at(slot)
            out = contract_last(unit[...], jnp.concatenate(split(rows[...]), axis=1))
            number = jnp.concatenate([samp[dev, i : i + 1] for i in range(lines)], axis=1)
            group = (number >> bits_of(table_rows)) & (LANES // SLOT - 1)
            sign = parity((number >> local_bits) & me, bits_of(devices))
            sign = (1 - 2 * sign).astype(jnp.float32) * scale
            total = jnp.zeros((used, per_dev), jnp.float32)
            for g in range(LANES // SLOT):
                total = jnp.where(group == g, out[g * SLOT : g * SLOT + used, :], total)
            total = total * sign
            main[slot] = total[:cols]
            for i in range(lines):
                last[pl.ds(slot * lines + i, 1), :] = total[cols : cols + 1, i * LANES : (i + 1) * LANES]

        def remote(src, dst, send_sem, recv_sem, peer):
            return pltpu.make_async_remote_copy(
                src_ref=src, dst_ref=dst, send_sem=send_sem, recv_sem=recv_sem,
                device_id=peer, device_id_type=MESH,
            )

        tall = n_quad * lines

        def group_of(k):
            return pl.ds(k * n_quad, n_quad), pl.ds(pl.multiple_of(k * tall, 8), tall)

        def mate_copies(k):
            at, at_last = group_of(k)
            return (
                remote(main.at[at], got_main.at[at], mate_sends.at[k], mate_recvs.at[k], mate),
                remote(
                    last.at[at_last], got_last.at[at_last],
                    mate_sends.at[chips + k], mate_recvs.at[chips + k], mate,
                ),
            )

        def chip_copies(k):
            at, at_last = group_of(k)
            peer = (chip_at(k) * 2 + core, quad)
            return (
                remote(sum_main.at[at], wide_main.at[k], chip_sends.at[k], chip_recvs.at[k], peer),
                remote(
                    sum_last.at[at_last], wide_last.at[k],
                    chip_sends.at[chips + k], chip_recvs.at[chips + k], peer,
                ),
            )

        fetch(0, picks_a, 0).start()
        fetch(1, picks_b, 1).start()
        fetch(0, picks_a, 0).wait()
        gather(picks_a, rows_a)
        fetch(2, picks_a, 0).start()
        pl.semaphore_wait(barrier, len(wide_peers) + len(quad_peers))

        def pair(i, carry):
            slot = 2 * i
            fetch(slot + 1, picks_b, 1).wait()
            gather(picks_b, rows_b)
            finish(slot, rows_a)
            fetch(slot + 3, picks_b, 1).start()
            fetch(slot + 2, picks_a, 0).wait()
            gather(picks_a, rows_a)
            finish(slot + 1, rows_b)
            fetch(slot + 4, picks_a, 0).start()
            return carry

        def step(k, carry):
            lax.fori_loop(k * n_quad // 2, (k + 1) * n_quad // 2, pair, 0)

            @pl.when(k < chips)
            def _():
                for copy in mate_copies(k):
                    copy.start()

            @pl.when(k >= chips)
            def _():
                own = k - chips
                for copy in mate_copies(own):
                    copy.wait_recv()
                at, at_last = group_of(own)
                from_at, from_last = group_of(k)
                sum_main[at] = main[from_at] + got_main[at]
                sum_last[at_last, :] = last[from_last, :] + got_last[at_last, :]

                @pl.when(own < chips - 1)
                def _():
                    for copy in chip_copies(own):
                        copy.start()

            return carry

        lax.fori_loop(0, 2 * chips, step, 0)
        fetch(0, picks_a, 0).wait()
        fetch(0, picks_b, 1).wait()
        for k in range(chips):
            for copy in mate_copies(k):
                copy.wait_send()
        for k in range(chips - 1):
            for copy in chip_copies(k):
                copy.wait()

        def add_row(to):
            row = sum_main[(chips - 1) * n_quad + to]
            for k in range(chips - 1):
                row = row + wide_main[k, to]
            row_main[to] = row

        sem_at = [0]

        def send(src, dst, peer):
            sem = sem_at[0]
            sem_at[0] += 1
            copy = remote(src, dst, sends.at[sem], recvs.at[sem], peer)
            copy.start()
            return copy

        ends = sum_last[(chips - 1) * tall :, :]
        for k in range(chips - 1):
            ends = ends + wide_last[k]
        row_last[...] = ends
        copies = []
        for k, peer in enumerate(quad_peers):
            add_row(peer[1])
            copies.append(send(row_main.at[peer[1]], quad_main.at[k], peer))
            copies.append(send(row_last, quad_last.at[k], peer))
        add_row(quad)
        for copy in copies:
            copy.wait()
        total = row_main[quad]
        ends = [row_last[pl.ds(quad * lines + i, 1), :] for i in range(lines)]
        for k in range(n_quad - 1):
            total = total + quad_main[k]
            ends = [e + quad_last[k, pl.ds(quad * lines + i, 1), :] for i, e in enumerate(ends)]
        end = jnp.concatenate(ends, axis=1)
        sketch[:cols, :] = total
        sketch[cols : cols + 1, :] = end

        group = jnp.concatenate([owners[me, i : i + 1] for i in range(lines)], axis=1)
        first = lax.broadcasted_iota(jnp.int32, (8, per_dev), 0) == 0
        right = jnp.concatenate([total, jnp.where(first, end, 0.0)], axis=0)
        left = jnp.concatenate([jnp.where(group == g, total, 0.0) for g in range(GROUPS)], axis=0)
        part = contract_last(right, left, precision=lax.Precision.HIGHEST)
        wide_gram[0] = part * (GROUPS / (per_dev * devices))
        copies = [send(wide_gram.at[0], wide_gram.at[k + 1], peer) for k, peer in enumerate(wide_peers)]
        for copy in copies:
            copy.wait()
        part = wide_gram[wide]
        for w in range(1, n_wide):
            part = part + wide_gram[(wide + n_wide - w) % n_wide]
        own_gram[...] = part
        copies = [send(own_gram, quad_gram.at[k], peer) for k, peer in enumerate(quad_peers)]
        for copy in copies:
            copy.wait()
        for k in range(n_quad - 1):
            part = part + quad_gram[k]
        gram[...] = part


def finish_kernel(n_quad, sketch_in, gram_in, sketch, gram, turned):
    quad = lax.axis_index("quad")
    owned, cols, _ = gram.shape
    sketch[...] = sketch_in[...]
    turned[:, : gram_in.shape[0]] = gram_in[...].T
    for g in range(owned):
        gram[g] = turned[pl.ds((quad * owned + g) * cols, cols), : cols + 1]


def shards(n_wide, n_quad, basis, target, sign_bits, samples, owners):
    cols, rows = basis.shape
    devices = n_wide * n_quad
    total_samples = samples.shape[0]
    per_dev = total_samples // devices
    lines = per_dev // LANES
    scale = 1.0 / math.sqrt(rows * devices)
    chunk = rows // HIGH
    mids = chunk // LINE
    vmem = pl.BlockSpec(memory_space=pltpu.VMEM)
    f32 = jnp.float32
    half, chips = devices // 2, n_wide // 2
    flat = (cols + 8, GROUPS * cols)
    spaces = [
        (devices, cols, per_dev), (devices * lines, LANES),
        (half, cols, per_dev), (half * lines, LANES),
        (half, cols, per_dev), (half * lines, LANES),
        (chips - 1, n_quad, cols, per_dev), (chips - 1, n_quad * lines, LANES),
        (n_quad, cols, per_dev), (n_quad * lines, LANES),
        (n_quad - 1, cols, per_dev), (n_quad - 1, n_quad * lines, LANES),
        (n_wide, *flat), flat, (n_quad - 1, *flat),
    ]
    copies = [2 * chips, 2 * chips, 3 * (n_quad - 1) + n_wide - 1]
    sketch, gram = pl.pallas_call(
        functools.partial(sketch_kernel, n_wide, n_quad, scale),
        grid=(HIGH,),
        out_shape=(
            jax.ShapeDtypeStruct((cols + 1, per_dev), f32),
            jax.ShapeDtypeStruct(flat, f32),
        ),
        in_specs=[
            vmem,
            vmem,
            pl.BlockSpec((chunk // LANES, LANES), lambda h: (h, 0)),
            pl.BlockSpec((cols, chunk), lambda h: (0, h)),
            pl.BlockSpec((chunk // LANES, LANES), lambda h: (h, 0)),
        ],
        out_specs=(vmem, vmem),
        scratch_shapes=[
            pltpu.VMEM((mids, HIGH * SLOT, LINE), f32),
            pltpu.VMEM((rows * SLOT // LANES, LANES), f32),
            pltpu.VMEM((LINE, 2 * LINE), jnp.bfloat16),
            pltpu.VMEM((LANES, 2 * LANES), jnp.bfloat16),
            pltpu.VMEM((devices, lines, LANES), jnp.int32),
            pltpu.SMEM((lines, LANES), jnp.int32),
            pltpu.SMEM((lines, LANES), jnp.int32),
            pltpu.VMEM((per_dev, LANES), f32),
            pltpu.VMEM((per_dev, LANES), f32),
            pltpu.SemaphoreType.DMA((2,)),
        ]
        + [pltpu.VMEM(space, f32) for space in spaces]
        + [pltpu.SemaphoreType.DMA((n,)) for n in copies for _ in range(2)],
        compiler_params=pltpu.CompilerParams(
            vmem_limit_bytes=60 * 1024 * 1024, collective_id=0, has_side_effects=True
        ),
    )(
        samples.reshape(devices, lines, LANES),
        owners.reshape(devices, lines, LANES),
        sign_bits.reshape(-1, LANES),
        basis,
        target.reshape(-1, LANES),
    )
    sketch, gram = pl.pallas_call(
        functools.partial(finish_kernel, n_quad),
        out_shape=(
            jax.ShapeDtypeStruct((cols + 1, per_dev), f32),
            jax.ShapeDtypeStruct((GROUPS // n_quad, cols, cols + 1), f32),
        ),
        in_specs=[vmem, vmem],
        out_specs=(vmem, vmem),
        scratch_shapes=[pltpu.VMEM((GROUPS * cols, LANES), f32)],
    )(sketch, gram)
    return sketch.T, gram


def solution(mesh):
    placed = (P(None, ("wide", "quad")), P(("wide", "quad")), P(("wide", "quad")), P(), P())
    return jax.shard_map(
        functools.partial(shards, mesh.shape["wide"], mesh.shape["quad"]),
        mesh=mesh,
        in_specs=placed,
        out_specs=(P(("wide", "quad"), None), P("quad", None, None)),
        check_vma=False,
    )
```

```python
import functools
import math

import jax
import jax.numpy as jnp
from jax import lax
from jax.experimental import pallas as pl
from jax.experimental.pallas import tpu as pltpu
from jax.sharding import PartitionSpec as P

GROUPS = 8
LANES = 128
LINE = 256
HIGH = 8
SLOT = 32
MESH = pl.DeviceIdType.MESH


def bits_of(n):
    return n.bit_length() - 1


def parity(x, nbits):
    shift = 1
    while shift < nbits:
        x = x ^ (x >> shift)
        shift *= 2
    return x & 1


def butterfly(parts):
    half = 1
    while half < len(parts):
        for at in range(0, len(parts), 2 * half):
            for i in range(at, at + half):
                parts[i], parts[i + half] = parts[i] + parts[i + half], parts[i] - parts[i + half]
        half *= 2
    return parts


def place_of(high):
    return ((high & 1) * (HIGH // 2) + (high >> 1)) * SLOT


def split(x):
    top = x.astype(jnp.bfloat16)
    return top, (x - top.astype(jnp.float32)).astype(jnp.bfloat16)


def contract_last(a, b, **kw):
    return lax.dot_general(a, b, (((1,), (1,)), ((), ())), preferred_element_type=jnp.float32, **kw)


def sketch_kernel(
    n_wide, n_quad, scale, samp, owners, bits_in, x_in, t_in, sketch, gram,
    bits_all, x_all, t_all, load_sems,
    field, table, walsh, unit, picks, picks_a, picks_b, rows_a, rows_b, sems,
    main, last, got_main, got_last, sum_main, sum_last, wide_main, wide_last,
    row_main, row_last, quad_main, quad_last, wide_gram, own_gram, quad_gram,
    mate_sends, mate_recvs, chip_sends, chip_recvs, sends, recvs
):
    chunk = x_all.shape[2]
    lines_in = chunk // LANES
    mids = chunk // LINE
    local_bits = bits_of(HIGH * chunk)
    devices, cols, per_dev = main.shape
    lines = per_dev // LANES
    wide = lax.axis_index("wide")
    quad = lax.axis_index("quad")
    me = wide * n_quad + quad
    core, chip, chips = wide % 2, wide // 2, n_wide // 2
    mate = (wide + 1 - 2 * core, quad)
    wide_peers = [((wide + k) % n_wide, quad) for k in range(1, n_wide)]
    quad_peers = [(wide, (quad + k) % n_quad) for k in range(1, n_quad)]
    barrier = pltpu.get_barrier_semaphore()

    def loads(h):
        at = pl.multiple_of(h * chunk, chunk)
        rows = pl.ds(pl.multiple_of(h * lines_in, lines_in), lines_in)
        return (
            pltpu.make_async_copy(bits_in.at[rows], bits_all.at[h], load_sems.at[0, h]),
            pltpu.make_async_copy(t_in.at[rows], t_all.at[h], load_sems.at[1, h]),
            pltpu.make_async_copy(x_in.at[:, pl.ds(at, chunk)], x_all.at[h], load_sems.at[2, h]),
        )

    for h in range(HIGH):
        for copy in loads(h):
            copy.start()
    for peer in wide_peers + quad_peers:
        pl.semaphore_signal(barrier, inc=1, device_id=peer, device_id_type=MESH)
    a = lax.broadcasted_iota(jnp.int32, (LINE, LINE), 0)
    b = lax.broadcasted_iota(jnp.int32, (LINE, LINE), 1)
    line = (1 - 2 * parity(a & b, bits_of(LINE))).astype(jnp.float32).astype(jnp.bfloat16)
    walsh[:, :LINE] = line
    walsh[:, LINE:] = line
    a = lax.broadcasted_iota(jnp.int32, (LANES, LANES), 0)
    b = lax.broadcasted_iota(jnp.int32, (LANES, LANES), 1)
    line = jnp.where(a == b, 1.0, 0.0).astype(jnp.bfloat16)
    unit[:, :LANES] = line
    unit[:, LANES:] = line
    picks[...] = samp[...] & (table.shape[0] - 1)

    row = lax.broadcasted_iota(jnp.int32, (8, LANES), 0)

    def first_pass(high, carry):
        for copy in loads(high):
            copy.wait()
        bits, t, x = bits_all.at[high], t_all.at[high], x_all.at[high]
        base = pl.multiple_of(place_of(high), SLOT)
        for part in range(LINE // LANES):
            for tile in range(cols // 8 + 1):
                values = []
                for mid in range(mids):
                    line = mid * (LINE // LANES) + part
                    flip = (1 - 2 * bits[line : line + 1, :]).astype(jnp.float32)
                    if tile < cols // 8:
                        value = x[tile * 8 : tile * 8 + 8, line * LANES : (line + 1) * LANES] * flip
                    else:
                        value = jnp.where(row == 0, t[line : line + 1, :] * flip, 0.0)
                    values.append(value)
                for mid, value in enumerate(butterfly(values)):
                    field[mid, pl.ds(base + tile * 8, 8), part * LANES : (part + 1) * LANES] = value
        return carry

    lax.fori_loop(0, HIGH, first_pass, 0)
    used = cols + 8

    def mix(mid, carry):
        halves = []
        for part in range(LINE // LANES):
            values = [
                field[mid, place_of(h) : place_of(h) + used, part * LANES : (part + 1) * LANES]
                for h in range(HIGH)
            ]
            values = butterfly(values)
            order = sorted(range(HIGH), key=place_of)
            blank = jnp.zeros((SLOT - used, LANES), jnp.float32)
            halves.append(jnp.concatenate([p for h in order for p in (values[h], blank)], axis=0))
        both = jnp.concatenate(split(jnp.concatenate(halves, axis=1)), axis=1)
        out = contract_last(walsh[...], both)
        at = pl.multiple_of(mid * LINE, LINE)
        table[pl.ds(at, LINE), :] = out[:, :LANES]
        table[pl.ds(at + mids * LINE, LINE), :] = out[:, LANES:]
        return carry

    lax.fori_loop(0, mids, mix, 0, unroll=4)
    table_rows = table.shape[0]
    half = devices // 2

    def chip_at(k):
        return (chip + 1 + k) % chips

    def device_at(slot):
        to_core = (core + 1 + slot // half) % 2
        to_wide = chip_at(slot // n_quad % chips) * 2 + to_core
        return to_wide * n_quad + slot % n_quad

    def fetch(slot, slots, sem):
        slot = jnp.minimum(slot, devices - 1)
        return pltpu.make_async_copy(picks.at[device_at(slot)], slots, sems.at[sem])

    def gather(slots, rows):
        for r in range(per_dev):
            rows[r : r + 1, :] = table[pl.ds(slots[r // LANES, r % LANES], 1), :]

    def finish(slot, rows):
        dev = device_at(slot)
        out = contract_last(unit[...], jnp.concatenate(split(rows[...]), axis=1))
        number = jnp.concatenate([samp[dev, i : i + 1] for i in range(lines)], axis=1)
        group = (number >> bits_of(table_rows)) & (LANES // SLOT - 1)
        sign = parity((number >> local_bits) & me, bits_of(devices))
        sign = (1 - 2 * sign).astype(jnp.float32) * scale
        total = jnp.zeros((used, per_dev), jnp.float32)
        for g in range(LANES // SLOT):
            total = jnp.where(group == g, out[g * SLOT : g * SLOT + used, :], total)
        total = total * sign
        main[slot] = total[:cols]
        for i in range(lines):
            last[pl.ds(slot * lines + i, 1), :] = total[cols : cols + 1, i * LANES : (i + 1) * LANES]

    def remote(src, dst, send_sem, recv_sem, peer):
        return pltpu.make_async_remote_copy(
            src_ref=src, dst_ref=dst, send_sem=send_sem, recv_sem=recv_sem,
            device_id=peer, device_id_type=MESH,
        )

    tall = n_quad * lines

    def group_of(k):
        return pl.ds(k * n_quad, n_quad), pl.ds(pl.multiple_of(k * tall, 8), tall)

    def mate_copies(k):
        at, at_last = group_of(k)
        return (
            remote(main.at[at], got_main.at[at], mate_sends.at[k], mate_recvs.at[k], mate),
            remote(
                last.at[at_last], got_last.at[at_last],
                mate_sends.at[chips + k], mate_recvs.at[chips + k], mate,
            ),
        )

    def chip_copies(k):
        at, at_last = group_of(k)
        peer = (chip_at(k) * 2 + core, quad)
        return (
            remote(sum_main.at[at], wide_main.at[k], chip_sends.at[k], chip_recvs.at[k], peer),
            remote(
                sum_last.at[at_last], wide_last.at[k],
                chip_sends.at[chips + k], chip_recvs.at[chips + k], peer,
            ),
        )

    fetch(0, picks_a, 0).start()
    fetch(1, picks_b, 1).start()
    fetch(0, picks_a, 0).wait()
    gather(picks_a, rows_a)
    fetch(2, picks_a, 0).start()
    pl.semaphore_wait(barrier, len(wide_peers) + len(quad_peers))

    def pair(i, carry):
        slot = 2 * i
        fetch(slot + 1, picks_b, 1).wait()
        gather(picks_b, rows_b)
        finish(slot, rows_a)
        fetch(slot + 3, picks_b, 1).start()
        fetch(slot + 2, picks_a, 0).wait()
        gather(picks_a, rows_a)
        finish(slot + 1, rows_b)
        fetch(slot + 4, picks_a, 0).start()
        return carry

    def step(k, carry):
        lax.fori_loop(k * n_quad // 2, (k + 1) * n_quad // 2, pair, 0)

        @pl.when(k < chips)
        def _():
            for copy in mate_copies(k):
                copy.start()

        @pl.when(k >= chips)
        def _():
            own = k - chips
            for copy in mate_copies(own):
                copy.wait_recv()
            at, at_last = group_of(own)
            from_at, from_last = group_of(k)
            sum_main[at] = main[from_at] + got_main[at]
            sum_last[at_last, :] = last[from_last, :] + got_last[at_last, :]

            @pl.when(own < chips - 1)
            def _():
                for copy in chip_copies(own):
                    copy.start()

        return carry

    lax.fori_loop(0, 2 * chips, step, 0)
    fetch(0, picks_a, 0).wait()
    fetch(0, picks_b, 1).wait()
    for k in range(chips):
        for copy in mate_copies(k):
            copy.wait_send()
    for k in range(chips - 1):
        for copy in chip_copies(k):
            copy.wait()

    def add_row(to):
        row = sum_main[(chips - 1) * n_quad + to]
        for k in range(chips - 1):
            row = row + wide_main[k, to]
        row_main[to] = row

    sem_at = [0]

    def send(src, dst, peer):
        sem = sem_at[0]
        sem_at[0] += 1
        copy = remote(src, dst, sends.at[sem], recvs.at[sem], peer)
        copy.start()
        return copy

    ends = sum_last[(chips - 1) * tall :, :]
    for k in range(chips - 1):
        ends = ends + wide_last[k]
    row_last[...] = ends
    copies = []
    for k, peer in enumerate(quad_peers):
        add_row(peer[1])
        copies.append(send(row_main.at[peer[1]], quad_main.at[k], peer))
        copies.append(send(row_last, quad_last.at[k], peer))
    add_row(quad)
    for copy in copies:
        copy.wait()
    total = row_main[quad]
    ends = [row_last[pl.ds(quad * lines + i, 1), :] for i in range(lines)]
    for k in range(n_quad - 1):
        total = total + quad_main[k]
        ends = [e + quad_last[k, pl.ds(quad * lines + i, 1), :] for i, e in enumerate(ends)]
    end = jnp.concatenate(ends, axis=1)
    sketch[:cols, :] = total
    sketch[cols : cols + 1, :] = end

    group = jnp.concatenate([owners[me, i : i + 1] for i in range(lines)], axis=1)
    first = lax.broadcasted_iota(jnp.int32, (8, per_dev), 0) == 0
    right = jnp.concatenate([total, jnp.where(first, end, 0.0)], axis=0)
    left = jnp.concatenate([jnp.where(group == g, total, 0.0) for g in range(GROUPS)], axis=0)
    part = contract_last(right, left, precision=lax.Precision.HIGHEST)
    part = part * (GROUPS / (per_dev * devices))
    span = GROUPS * cols // n_quad
    block = lax.broadcasted_iota(jnp.int32, (8, LANES), 1) // span
    for q in range(n_quad):
        packed = jnp.zeros((8, LANES), jnp.float32)
        for tile in range(part.shape[0] // 8):
            turned = part[tile * 8 : tile * 8 + 8, :]
            if (tile - q) % n_quad:
                turned = pltpu.roll(turned, (tile - q) % n_quad * span, 1)
            packed = jnp.where(block == tile, turned, packed)
        own_gram[q] = packed
    copies = [send(own_gram.at[peer[1]], quad_gram.at[k], peer) for k, peer in enumerate(quad_peers)]
    for copy in copies:
        copy.wait()
    packed = own_gram[quad]
    for k in range(n_quad - 1):
        packed = packed + quad_gram[k]
    wide_gram[0] = packed
    copies = [send(wide_gram.at[0], wide_gram.at[k + 1], peer) for k, peer in enumerate(wide_peers)]
    for copy in copies:
        copy.wait()
    packed = wide_gram[wide]
    for w in range(1, n_wide):
        packed = packed + wide_gram[(wide + n_wide - w) % n_wide]
    gram[...] = packed


def finish_kernel(sketch_in, gram_in, sketch, gram):
    owned, cols, width = gram.shape
    sketch[...] = sketch_in[...]
    turned = gram_in[...].T
    for tile in range(-(-width // 8)):
        columns = min(8, width - tile * 8)
        for g in range(owned):
            at = (tile * owned + g) * cols
            gram[g, :, tile * 8 : tile * 8 + columns] = turned[at : at + cols, :columns]


def shards(n_wide, n_quad, basis, target, sign_bits, samples, owners):
    cols, rows = basis.shape
    devices = n_wide * n_quad
    total_samples = samples.shape[0]
    per_dev = total_samples // devices
    lines = per_dev // LANES
    scale = 1.0 / math.sqrt(rows * devices)
    chunk = rows // HIGH
    mids = chunk // LINE
    vmem = pl.BlockSpec(memory_space=pltpu.VMEM)
    f32 = jnp.float32
    half, chips = devices // 2, n_wide // 2
    flat = (8, LANES)
    spaces = [
        (devices, cols, per_dev), (devices * lines, LANES),
        (half, cols, per_dev), (half * lines, LANES),
        (half, cols, per_dev), (half * lines, LANES),
        (chips - 1, n_quad, cols, per_dev), (chips - 1, n_quad * lines, LANES),
        (n_quad, cols, per_dev), (n_quad * lines, LANES),
        (n_quad - 1, cols, per_dev), (n_quad - 1, n_quad * lines, LANES),
        (n_wide, *flat), (n_quad, *flat), (n_quad - 1, *flat),
    ]
    copies = [2 * chips, 2 * chips, 3 * (n_quad - 1) + n_wide - 1]
    sketch, gram = pl.pallas_call(
        functools.partial(sketch_kernel, n_wide, n_quad, scale),
        out_shape=(
            jax.ShapeDtypeStruct((cols + 1, per_dev), f32),
            jax.ShapeDtypeStruct(flat, f32),
        ),
        in_specs=[
            vmem,
            vmem,
            pl.BlockSpec(memory_space=pl.ANY),
            pl.BlockSpec(memory_space=pl.ANY),
            pl.BlockSpec(memory_space=pl.ANY),
        ],
        out_specs=(vmem, vmem),
        scratch_shapes=[
            pltpu.VMEM((HIGH, chunk // LANES, LANES), jnp.int32),
            pltpu.VMEM((HIGH, cols, chunk), f32),
            pltpu.VMEM((HIGH, chunk // LANES, LANES), f32),
            pltpu.SemaphoreType.DMA((3, HIGH)),
            pltpu.VMEM((mids, HIGH * SLOT, LINE), f32),
            pltpu.VMEM((rows * SLOT // LANES, LANES), f32),
            pltpu.VMEM((LINE, 2 * LINE), jnp.bfloat16),
            pltpu.VMEM((LANES, 2 * LANES), jnp.bfloat16),
            pltpu.VMEM((devices, lines, LANES), jnp.int32),
            pltpu.SMEM((lines, LANES), jnp.int32),
            pltpu.SMEM((lines, LANES), jnp.int32),
            pltpu.VMEM((per_dev, LANES), f32),
            pltpu.VMEM((per_dev, LANES), f32),
            pltpu.SemaphoreType.DMA((2,)),
        ]
        + [pltpu.VMEM(space, f32) for space in spaces]
        + [pltpu.SemaphoreType.DMA((n,)) for n in copies for _ in range(2)],
        compiler_params=pltpu.CompilerParams(
            vmem_limit_bytes=60 * 1024 * 1024, collective_id=0, has_side_effects=True
        ),
    )(
        samples.reshape(devices, lines, LANES),
        owners.reshape(devices, lines, LANES),
        sign_bits.reshape(-1, LANES),
        basis,
        target.reshape(-1, LANES),
    )
    sketch, gram = pl.pallas_call(
        finish_kernel,
        out_shape=(
            jax.ShapeDtypeStruct((cols + 1, per_dev), f32),
            jax.ShapeDtypeStruct((GROUPS // n_quad, cols, cols + 1), f32),
        ),
        in_specs=[vmem, vmem],
        out_specs=(vmem, vmem),
    )(sketch, gram)
    return sketch.T, gram


def solution(mesh):
    placed = (P(None, ("wide", "quad")), P(("wide", "quad")), P(("wide", "quad")), P(), P())
    return jax.shard_map(
        functools.partial(shards, mesh.shape["wide"], mesh.shape["quad"]),
        mesh=mesh,
        in_specs=placed,
        out_specs=(P(("wide", "quad"), None), P("quad", None, None)),
        check_vma=False,
    )
```

```python
import functools
import math

import jax
import jax.numpy as jnp
from jax import lax
from jax.experimental import pallas as pl
from jax.experimental.pallas import tpu as pltpu
from jax.sharding import PartitionSpec as P

GROUPS = 8
LANES = 128
LINE = 256
HIGH = 8
SLOT = 32
MESH = pl.DeviceIdType.MESH


def bits_of(n):
    return n.bit_length() - 1


def parity(x, nbits):
    shift = 1
    while shift < nbits:
        x = x ^ (x >> shift)
        shift *= 2
    return x & 1


def butterfly(parts):
    half = 1
    while half < len(parts):
        for at in range(0, len(parts), 2 * half):
            for i in range(at, at + half):
                parts[i], parts[i + half] = parts[i] + parts[i + half], parts[i] - parts[i + half]
        half *= 2
    return parts


def place_of(high):
    return ((high & 1) * (HIGH // 2) + (high >> 1)) * SLOT


def split(x):
    top = x.astype(jnp.bfloat16)
    return top, (x - top.astype(jnp.float32)).astype(jnp.bfloat16)


def contract_last(a, b, **kw):
    return lax.dot_general(a, b, (((1,), (1,)), ((), ())), preferred_element_type=jnp.float32, **kw)


def sketch_kernel(
    n_wide, n_quad, scale, samp, owners, bits_in, x_in, t_in, sketch, gram,
    bits_all, x_all, t_all, load_sems,
    field, table, walsh, unit, picks, picks_a, picks_b, rows_a, rows_b, sems,
    main, last, got_main, got_last, sum_main, sum_last, wide_main, wide_last,
    row_main, row_last, quad_main, quad_last, wide_gram, own_gram, quad_gram,
    mate_sends, mate_recvs, chip_sends, chip_recvs, sends, recvs
):
    chunk = x_all.shape[2]
    lines_in = chunk // LANES
    mids = chunk // LINE
    local_bits = bits_of(HIGH * chunk)
    devices, cols, per_dev = main.shape
    lines = per_dev // LANES
    wide = lax.axis_index("wide")
    quad = lax.axis_index("quad")
    me = wide * n_quad + quad
    core, chip, chips = wide % 2, wide // 2, n_wide // 2
    mate = (wide + 1 - 2 * core, quad)
    wide_peers = [((wide + k) % n_wide, quad) for k in range(1, n_wide)]
    quad_peers = [(wide, (quad + k) % n_quad) for k in range(1, n_quad)]
    barrier = pltpu.get_barrier_semaphore()

    def loads(h):
        at = pl.multiple_of(h * chunk, chunk)
        rows = pl.ds(pl.multiple_of(h * lines_in, lines_in), lines_in)
        return (
            pltpu.make_async_copy(bits_in.at[rows], bits_all.at[h], load_sems.at[0, h]),
            pltpu.make_async_copy(t_in.at[rows], t_all.at[h], load_sems.at[1, h]),
            pltpu.make_async_copy(x_in.at[:, pl.ds(at, chunk)], x_all.at[h], load_sems.at[2, h]),
        )

    for h in range(HIGH):
        for copy in loads(h):
            copy.start()
    for peer in wide_peers + quad_peers:
        pl.semaphore_signal(barrier, inc=1, device_id=peer, device_id_type=MESH)
    a = lax.broadcasted_iota(jnp.int32, (LINE, LINE), 0)
    b = lax.broadcasted_iota(jnp.int32, (LINE, LINE), 1)
    line = (1 - 2 * parity(a & b, bits_of(LINE))).astype(jnp.float32).astype(jnp.bfloat16)
    walsh[:, :LINE] = line
    walsh[:, LINE:] = line
    a = lax.broadcasted_iota(jnp.int32, (LANES, LANES), 0)
    b = lax.broadcasted_iota(jnp.int32, (LANES, LANES), 1)
    line = jnp.where(a == b, 1.0, 0.0).astype(jnp.bfloat16)
    unit[:, :LANES] = line
    unit[:, LANES:] = line
    picks[...] = samp[...] & (table.shape[0] - 1)

    row = lax.broadcasted_iota(jnp.int32, (8, LANES), 0)

    def first_pass(high, carry):
        for copy in loads(high):
            copy.wait()
        bits, t, x = bits_all.at[high], t_all.at[high], x_all.at[high]
        base = pl.multiple_of(place_of(high), SLOT)
        for part in range(LINE // LANES):
            for tile in range(cols // 8 + 1):
                values = []
                for mid in range(mids):
                    line = mid * (LINE // LANES) + part
                    flip = (1 - 2 * bits[line : line + 1, :]).astype(jnp.float32)
                    if tile < cols // 8:
                        value = x[tile * 8 : tile * 8 + 8, line * LANES : (line + 1) * LANES] * flip
                    else:
                        value = jnp.where(row == 0, t[line : line + 1, :] * flip, 0.0)
                    values.append(value)
                for mid, value in enumerate(butterfly(values)):
                    field[mid, pl.ds(base + tile * 8, 8), part * LANES : (part + 1) * LANES] = value
        return carry

    lax.fori_loop(0, HIGH, first_pass, 0)
    used = cols + 8

    def mix(mid, carry):
        halves = []
        for part in range(LINE // LANES):
            values = [
                field[mid, place_of(h) : place_of(h) + used, part * LANES : (part + 1) * LANES]
                for h in range(HIGH)
            ]
            values = butterfly(values)
            order = sorted(range(HIGH), key=place_of)
            blank = jnp.zeros((SLOT - used, LANES), jnp.float32)
            halves.append(jnp.concatenate([p for h in order for p in (values[h], blank)], axis=0))
        both = jnp.concatenate(split(jnp.concatenate(halves, axis=1)), axis=1)
        out = contract_last(walsh[...], both)
        at = pl.multiple_of(mid * LINE, LINE)
        table[pl.ds(at, LINE), :] = out[:, :LANES]
        table[pl.ds(at + mids * LINE, LINE), :] = out[:, LANES:]
        return carry

    lax.fori_loop(0, mids, mix, 0, unroll=8)
    table_rows = table.shape[0]
    half = devices // 2

    def chip_at(k):
        return (chip + 1 + k) % chips

    def device_at(slot):
        to_core = (core + 1 + slot // half) % 2
        to_wide = chip_at(slot // n_quad % chips) * 2 + to_core
        return to_wide * n_quad + slot % n_quad

    def fetch(slot, slots, sem):
        slot = jnp.minimum(slot, devices - 1)
        return pltpu.make_async_copy(picks.at[device_at(slot)], slots, sems.at[sem])

    def gather(slots, rows):
        for r in range(per_dev):
            rows[r : r + 1, :] = table[pl.ds(slots[r // LANES, r % LANES], 1), :]

    def finish(slot, rows):
        dev = device_at(slot)
        out = contract_last(unit[...], jnp.concatenate(split(rows[...]), axis=1))
        number = jnp.concatenate([samp[dev, i : i + 1] for i in range(lines)], axis=1)
        group = (number >> bits_of(table_rows)) & (LANES // SLOT - 1)
        sign = parity((number >> local_bits) & me, bits_of(devices))
        sign = (1 - 2 * sign).astype(jnp.float32) * scale
        total = jnp.zeros((used, per_dev), jnp.float32)
        for g in range(LANES // SLOT):
            total = jnp.where(group == g, out[g * SLOT : g * SLOT + used, :], total)
        total = total * sign
        main[slot] = total[:cols]
        for i in range(lines):
            last[pl.ds(slot * lines + i, 1), :] = total[cols : cols + 1, i * LANES : (i + 1) * LANES]

    def remote(src, dst, send_sem, recv_sem, peer):
        return pltpu.make_async_remote_copy(
            src_ref=src, dst_ref=dst, send_sem=send_sem, recv_sem=recv_sem,
            device_id=peer, device_id_type=MESH,
        )

    tall = n_quad * lines

    def group_of(k):
        return pl.ds(k * n_quad, n_quad), pl.ds(pl.multiple_of(k * tall, 8), tall)

    def mate_copies(k):
        at, at_last = group_of(k)
        return (
            remote(main.at[at], got_main.at[at], mate_sends.at[k], mate_recvs.at[k], mate),
            remote(
                last.at[at_last], got_last.at[at_last],
                mate_sends.at[chips + k], mate_recvs.at[chips + k], mate,
            ),
        )

    def chip_copies(k):
        at, at_last = group_of(k)
        peer = (chip_at(k) * 2 + core, quad)
        return (
            remote(sum_main.at[at], wide_main.at[k], chip_sends.at[k], chip_recvs.at[k], peer),
            remote(
                sum_last.at[at_last], wide_last.at[k],
                chip_sends.at[chips + k], chip_recvs.at[chips + k], peer,
            ),
        )

    fetch(0, picks_a, 0).start()
    fetch(1, picks_b, 1).start()
    fetch(0, picks_a, 0).wait()
    gather(picks_a, rows_a)
    fetch(2, picks_a, 0).start()
    pl.semaphore_wait(barrier, len(wide_peers) + len(quad_peers))

    def pair(i, carry):
        slot = 2 * i
        fetch(slot + 1, picks_b, 1).wait()
        gather(picks_b, rows_b)
        finish(slot, rows_a)
        fetch(slot + 3, picks_b, 1).start()
        fetch(slot + 2, picks_a, 0).wait()
        gather(picks_a, rows_a)
        finish(slot + 1, rows_b)
        fetch(slot + 4, picks_a, 0).start()
        return carry

    def step(k, carry):
        lax.fori_loop(k * n_quad // 2, (k + 1) * n_quad // 2, pair, 0)

        @pl.when(k < chips)
        def _():
            for copy in mate_copies(k):
                copy.start()

        @pl.when(k >= chips)
        def _():
            own = k - chips
            for copy in mate_copies(own):
                copy.wait_recv()
            at, at_last = group_of(own)
            from_at, from_last = group_of(k)
            sum_main[at] = main[from_at] + got_main[at]
            sum_last[at_last, :] = last[from_last, :] + got_last[at_last, :]

            @pl.when(own < chips - 1)
            def _():
                for copy in chip_copies(own):
                    copy.start()

        return carry

    lax.fori_loop(0, 2 * chips, step, 0)
    fetch(0, picks_a, 0).wait()
    fetch(0, picks_b, 1).wait()
    for k in range(chips):
        for copy in mate_copies(k):
            copy.wait_send()
    for k in range(chips - 1):
        for copy in chip_copies(k):
            copy.wait()

    def add_row(to):
        row = sum_main[(chips - 1) * n_quad + to]
        for k in range(chips - 1):
            row = row + wide_main[k, to]
        row_main[to] = row

    sem_at = [0]

    def send(src, dst, peer):
        sem = sem_at[0]
        sem_at[0] += 1
        copy = remote(src, dst, sends.at[sem], recvs.at[sem], peer)
        copy.start()
        return copy

    ends = sum_last[(chips - 1) * tall :, :]
    for k in range(chips - 1):
        ends = ends + wide_last[k]
    row_last[...] = ends
    copies = []
    for k, peer in enumerate(quad_peers):
        add_row(peer[1])
        copies.append(send(row_main.at[peer[1]], quad_main.at[k], peer))
        copies.append(send(row_last, quad_last.at[k], peer))
    add_row(quad)
    for copy in copies:
        copy.wait()
    total = row_main[quad]
    ends = [row_last[pl.ds(quad * lines + i, 1), :] for i in range(lines)]
    for k in range(n_quad - 1):
        total = total + quad_main[k]
        ends = [e + quad_last[k, pl.ds(quad * lines + i, 1), :] for i, e in enumerate(ends)]
    end = jnp.concatenate(ends, axis=1)
    sketch[:cols, :] = total
    sketch[cols : cols + 1, :] = end

    group = jnp.concatenate([owners[me, i : i + 1] for i in range(lines)], axis=1)
    first = lax.broadcasted_iota(jnp.int32, (8, per_dev), 0) == 0
    right = jnp.concatenate([total, jnp.where(first, end, 0.0)], axis=0)
    left = jnp.concatenate([jnp.where(group == g, total, 0.0) for g in range(GROUPS)], axis=0)
    part = contract_last(right, left, precision=lax.Precision.HIGHEST)
    part = part * (GROUPS / (per_dev * devices))
    span = GROUPS * cols // n_quad
    block = lax.broadcasted_iota(jnp.int32, (8, LANES), 1) // span
    for q in range(n_quad):
        packed = jnp.zeros((8, LANES), jnp.float32)
        for tile in range(part.shape[0] // 8):
            turned = part[tile * 8 : tile * 8 + 8, :]
            if (tile - q) % n_quad:
                turned = pltpu.roll(turned, (tile - q) % n_quad * span, 1)
            packed = jnp.where(block == tile, turned, packed)
        own_gram[q] = packed
    copies = [send(own_gram.at[peer[1]], quad_gram.at[k], peer) for k, peer in enumerate(quad_peers)]
    for copy in copies:
        copy.wait()
    packed = own_gram[quad]
    for k in range(n_quad - 1):
        packed = packed + quad_gram[k]
    wide_gram[0] = packed
    copies = [send(wide_gram.at[0], wide_gram.at[k + 1], peer) for k, peer in enumerate(wide_peers)]
    for copy in copies:
        copy.wait()
    packed = wide_gram[wide]
    for w in range(1, n_wide):
        packed = packed + wide_gram[(wide + n_wide - w) % n_wide]
    gram[...] = packed


def finish_kernel(sketch_in, gram_in, sketch, gram):
    owned, cols, width = gram.shape
    sketch[...] = sketch_in[...]
    turned = gram_in[...].T
    for tile in range(-(-width // 8)):
        columns = min(8, width - tile * 8)
        for g in range(owned):
            at = (tile * owned + g) * cols
            gram[g, :, tile * 8 : tile * 8 + columns] = turned[at : at + cols, :columns]


def shards(n_wide, n_quad, basis, target, sign_bits, samples, owners):
    cols, rows = basis.shape
    devices = n_wide * n_quad
    total_samples = samples.shape[0]
    per_dev = total_samples // devices
    lines = per_dev // LANES
    scale = 1.0 / math.sqrt(rows * devices)
    chunk = rows // HIGH
    mids = chunk // LINE
    vmem = pl.BlockSpec(memory_space=pltpu.VMEM)
    f32 = jnp.float32
    half, chips = devices // 2, n_wide // 2
    flat = (8, LANES)
    spaces = [
        (devices, cols, per_dev), (devices * lines, LANES),
        (half, cols, per_dev), (half * lines, LANES),
        (half, cols, per_dev), (half * lines, LANES),
        (chips - 1, n_quad, cols, per_dev), (chips - 1, n_quad * lines, LANES),
        (n_quad, cols, per_dev), (n_quad * lines, LANES),
        (n_quad - 1, cols, per_dev), (n_quad - 1, n_quad * lines, LANES),
        (n_wide, *flat), (n_quad, *flat), (n_quad - 1, *flat),
    ]
    copies = [2 * chips, 2 * chips, 3 * (n_quad - 1) + n_wide - 1]
    sketch, gram = pl.pallas_call(
        functools.partial(sketch_kernel, n_wide, n_quad, scale),
        out_shape=(
            jax.ShapeDtypeStruct((cols + 1, per_dev), f32),
            jax.ShapeDtypeStruct(flat, f32),
        ),
        in_specs=[
            vmem,
            vmem,
            pl.BlockSpec(memory_space=pl.ANY),
            pl.BlockSpec(memory_space=pl.ANY),
            pl.BlockSpec(memory_space=pl.ANY),
        ],
        out_specs=(vmem, vmem),
        scratch_shapes=[
            pltpu.VMEM((HIGH, chunk // LANES, LANES), jnp.int32),
            pltpu.VMEM((HIGH, cols, chunk), f32),
            pltpu.VMEM((HIGH, chunk // LANES, LANES), f32),
            pltpu.SemaphoreType.DMA((3, HIGH)),
            pltpu.VMEM((mids, HIGH * SLOT, LINE), f32),
            pltpu.VMEM((rows * SLOT // LANES, LANES), f32),
            pltpu.VMEM((LINE, 2 * LINE), jnp.bfloat16),
            pltpu.VMEM((LANES, 2 * LANES), jnp.bfloat16),
            pltpu.VMEM((devices, lines, LANES), jnp.int32),
            pltpu.SMEM((lines, LANES), jnp.int32),
            pltpu.SMEM((lines, LANES), jnp.int32),
            pltpu.VMEM((per_dev, LANES), f32),
            pltpu.VMEM((per_dev, LANES), f32),
            pltpu.SemaphoreType.DMA((2,)),
        ]
        + [pltpu.VMEM(space, f32) for space in spaces]
        + [pltpu.SemaphoreType.DMA((n,)) for n in copies for _ in range(2)],
        compiler_params=pltpu.CompilerParams(
            vmem_limit_bytes=60 * 1024 * 1024, collective_id=0, has_side_effects=True
        ),
    )(
        samples.reshape(devices, lines, LANES),
        owners.reshape(devices, lines, LANES),
        sign_bits.reshape(-1, LANES),
        basis,
        target.reshape(-1, LANES),
    )
    sketch, gram = pl.pallas_call(
        finish_kernel,
        out_shape=(
            jax.ShapeDtypeStruct((cols + 1, per_dev), f32),
            jax.ShapeDtypeStruct((GROUPS // n_quad, cols, cols + 1), f32),
        ),
        in_specs=[vmem, vmem],
        out_specs=(vmem, vmem),
    )(sketch, gram)
    return sketch.T, gram


def solution(mesh):
    placed = (P(None, ("wide", "quad")), P(("wide", "quad")), P(("wide", "quad")), P(), P())
    return jax.shard_map(
        functools.partial(shards, mesh.shape["wide"], mesh.shape["quad"]),
        mesh=mesh,
        in_specs=placed,
        out_specs=(P(("wide", "quad"), None), P("quad", None, None)),
        check_vma=False,
    )
```
